512 devices in a mesh: space: 16 (over z), chaos: 32 (over y, x, core).
Axes of the slice: x: 4, y: 4, z: 16, core: 2. Of those that a mesh axis runs over, the one named last changes fastest.
Arguments:
- field: float32 [1792, 32, 8, 128], P('chaos', 'space'), may hold values from -6 to 6
- modes: float32 [21, 32, 8, 128], P(None, 'space'), may hold values from -6 to 6
- send_rows: int32 [32, 256], P('chaos'), may hold values from 0 to 55, as said below
- pick: int32 [1792, 41], P('chaos'), may hold values from 0 to 255
- mode_ids: int32 [1792, 41], P('chaos'), may hold values from 0 to 20
- coef: float32 [1792, 41], P('chaos'), may hold values from -0.15 to 0.15
Outputs:
- first: float32 [1792, 32, 8, 128], P('chaos', 'space')
- second: float32 [1792, 32, 8, 128], P('chaos', 'space')
The draws below stay inside these ranges and needn't reach their ends.
Inputs may be any that keep to these rules, and one draw needn't show every extreme that they name: `send_rows`: in row e, each block of 8 entries d * 8 to d * 8 + 7 holds different local terms of owner e.
All inputs are finite; a program needn't handle non-finite values.
Results may differ from the reference program's by a relative error of at most 0.000098.
Values sent between devices are 32-bit elements; how exact they have to be, the bound alone decides.
A program may use at most 64 MiB of HBM per device.

```python
import jax
import jax.numpy as jnp
from jax import lax

MODES = 21
TERMS_DEV = 56
SLOTS = 41
CAP = 8
GX = 8
GY = 128
GROUPS = 32
TERMS = 1792
POOL = 256
NZ = 32


def draw_send_rows(key, part):
    keys = jax.random.split(key, GROUPS * GROUPS)
    lists = jax.vmap(lambda single: jax.random.permutation(single, TERMS_DEV)[:CAP])(keys)
    return lists.reshape(GROUPS, GROUPS * CAP).astype(jnp.int32)


def place_ends(entries, own_key, least, top_value):
    dims = entries.shape
    index_at = [jax.random.randint(jax.random.fold_in(own_key, axis), (), 0, dims[axis]) for axis in range(len(dims))]
    entries = entries.at[tuple(index_at)].set(least)
    longest = dims.index(max(dims))
    index_at[longest] = (index_at[longest] + 1) % dims[longest]
    return entries.at[tuple(index_at)].set(top_value)


def block_levels(key, extent, shards, low, high):
    def one(position, blocks):
        heights = jax.random.uniform(jax.random.fold_in(jax.random.fold_in(key, 6), position), (blocks,), jnp.float32, low / len(shards), high / len(shards))
        return jnp.repeat(jnp.exp(heights), extent[position] // blocks).reshape((-1,) + (1,) * (len(extent) - position - 1))

    factor_of = one(*shards[0])
    for cut in shards[1:]:
        factor_of = factor_of * one(*cut)
    return factor_of


def normal_values(stream_key, extent, width, most, cuts=(), kind=jnp.bfloat16):
    array = width * jax.random.normal(stream_key, extent, jnp.float32)
    if cuts:
        array = array * block_levels(stream_key, extent, cuts, -0.22, 0.18)
    return jnp.clip(array, -most, most).astype(kind)


def setup_inputs(seed: int = 0) -> dict:
    key_list = jax.random.split(jax.random.key(seed), 7)
    return {
        "field": normal_values(key_list[0], (TERMS, NZ, GX, GY), 1.0, 6.0, ((0, 32), (1, 16)), jnp.float32),
        "modes": normal_values(key_list[1], (MODES, NZ, GX, GY), 1.0, 6.0, ((1, 16),), jnp.float32),
        "send_rows": draw_send_rows(jax.random.fold_in(key_list[6], 71), 0),
        "pick": place_ends(jax.random.randint(key_list[3], (TERMS, SLOTS), 0, POOL), jax.random.fold_in(key_list[3], 1), 0, POOL - 1).astype(jnp.int32),
        "mode_ids": place_ends(jax.random.randint(key_list[4], (TERMS, SLOTS), 0, MODES), jax.random.fold_in(key_list[4], 1), 0, MODES - 1).astype(jnp.int32),
        "coef": normal_values(key_list[5], (TERMS, SLOTS), 0.025, 0.15, ((0, 32),), jnp.float32),
    }


def laplace(padded):
    center = padded[:, 1:-1]
    side = jnp.pad(center, ((0, 0), (0, 0), (1, 1), (1, 1)))
    beside = padded[:, 2:] + padded[:, :-2]
    beside = beside + side[:, :, 2:, 1:-1] + side[:, :, :-2, 1:-1]
    beside = beside + side[:, :, 1:-1, 2:] + side[:, :, 1:-1, :-2]
    return 6.0 * center - beside


def reference(field, modes, send_rows, pick, mode_ids, coef):
    owner = (jnp.arange(TERMS, dtype=jnp.int32) // TERMS_DEV)[:, None]
    source = pick // CAP
    within = pick % CAP
    local_rows = send_rows[source, owner * CAP + within]
    column = (source * TERMS_DEV + local_rows).astype(jnp.int32)
    flat_modes = modes.reshape(MODES, -1)

    def apply(values):
        padded = jnp.pad(values, ((0, 0), (1, 1), (0, 0), (0, 0)))
        images = laplace(padded).reshape(TERMS, -1)

        def one_row(packed):
            cols, mds, cfs = packed
            return jnp.sum(cfs[:, None] * images[cols] * flat_modes[mds], axis=0)

        return lax.map(one_row, (column, mode_ids, coef)).reshape(values.shape)

    first = apply(field)
    second = apply(first)
    return (first, second)
```

```python
import functools

import jax
import jax.numpy as jnp
from jax import lax
from jax.experimental import pallas as pl
from jax.experimental.pallas import tpu as pltpu
from jax.sharding import PartitionSpec as P

f32 = jnp.float32
bf16 = jnp.bfloat16
MESH = pl.DeviceIdType.MESH

SPACE = 16
OWNERS = 32
SIDE = 4
TERMS = 56
CAP = 8
POOL = OWNERS * CAP
SLOTS = 41
MODES = 21
MODES_PAD = 24
PLANES = 2
GX = 8
GY = 128
CELL_ROWS = GX * PLANES
W_ROWS = 1184
AWAY = OWNERS - 1

FIRST_STEPS = ((0, 4), (4, 8))
SECOND_STEPS = ((0, 3), (3, 6), (6, 8))
HALO_STEPS = ((0, 4), (4, 8))


def _offsets():
    far = lambda n: min(n, SIDE - n)
    every = [
        (dy, dx, dc)
        for dy in range(SIDE)
        for dx in range(SIDE)
        for dc in range(2)
        if (dy, dx, dc) != (0, 0, 0)
    ]
    return sorted(every, key=lambda t: -(far(t[0]) + far(t[1])))


def _lanes(values):
    lane = lax.broadcasted_iota(jnp.int32, values.shape, 1)
    after = jnp.where(lane == GY - 1, 0.0, pltpu.roll(values, GY - 1, axis=1))
    before = jnp.where(lane == 0, 0.0, pltpu.roll(values, 1, axis=1))
    return after + before


def _laplace(lo, hi, low_ref, high_ref, has_low, has_high, terms, lap):
    for g in range(lo, hi):
        for p in range(PLANES):
            center = terms[g, p]
            if p == 0:
                outer = jnp.where(has_low, low_ref[g], 0.0)
            else:
                outer = jnp.where(has_high, high_ref[g], 0.0)
            beside = terms[g, 1 - p] + outer + _lanes(center)
            if g > 0:
                beside = beside + terms[g - 1, p]
            if g < GX - 1:
                beside = beside + terms[g + 1, p]
            lap[pl.ds((g * PLANES + p) * TERMS, TERMS), :] = 6.0 * center - beside


def _weights(pick_ref, mid_ref, coef_ref, wf, wcat):
    def row(i, carry):
        picked = pick_ref[pl.ds(i, 1), :]
        mode = mid_ref[pl.ds(i, 1), :]
        coef = coef_ref[pl.ds(i, 1), :]
        which = jnp.where(
            lax.broadcasted_iota(jnp.int32, (MODES_PAD, SLOTS), 0) == mode, coef, 0.0
        )
        place = jnp.where(
            lax.broadcasted_iota(jnp.int32, (POOL, SLOTS), 0) == picked, 1.0, 0.0
        ).astype(bf16)
        top = which.astype(bf16)
        rest = which - top.astype(f32)
        mid = rest.astype(bf16)
        low = (rest - mid.astype(f32)).astype(bf16)
        parts = lax.dot_general(
            jnp.concatenate([top, mid, low], axis=0),
            place,
            (((1,), (1,)), ((), ())),
            preferred_element_type=f32,
        )
        n = MODES_PAD
        total = parts[0:n] + (parts[n : 2 * n] + parts[2 * n : 3 * n])
        wf[0, pl.ds(i, n, stride=TERMS), :] = total[:, 0:128]
        wf[1, pl.ds(i, n, stride=TERMS), :] = total[:, 128:256]
        return carry

    lax.fori_loop(0, TERMS, row, 0)

    def split(t, carry):
        at = pl.multiple_of(t * 16, 16)
        for h in range(2):
            w = wf[h, pl.ds(at, 16), :]
            top = w.astype(bf16)
            low = (w - top.astype(f32)).astype(bf16)
            wcat[pl.ds(at, 16), h * 128 : (h + 1) * 128] = top
            wcat[pl.ds(at, 16), POOL + h * 128 : POOL + (h + 1) * 128] = top
            wcat[pl.ds(at, 16), 2 * POOL + h * 128 : 2 * POOL + (h + 1) * 128] = low
        return carry

    lax.fori_loop(0, W_ROWS // 16, split, 0)


def _mix(lo, hi, pool, wcat, modes, mixed, out, terms):
    def one(g, carry):
        images = jnp.concatenate(
            [
                pool[pl.ds(pl.multiple_of(g * PLANES * POOL, POOL), POOL), :],
                pool[pl.ds(pl.multiple_of(g * PLANES * POOL + POOL, POOL), POOL), :],
            ],
            axis=1,
        )
        top = images.astype(bf16)
        low = (images - top.astype(f32)).astype(bf16)
        mixed[...] = jnp.dot(
            wcat[...], jnp.concatenate([top, low, top], axis=0), preferred_element_type=f32
        )
        for p in range(PLANES):
            total = None
            for k in range(MODES):
                scale = modes[pl.ds(k * CELL_ROWS + p * GX + g, 1), :]
                part = mixed[k * TERMS : (k + 1) * TERMS, p * GY : (p + 1) * GY] * scale
                total = part if total is None else total + part
            out[pl.ds(p * GX + g, TERMS, stride=CELL_ROWS), :] = total
            if terms is not None:
                terms[g, p] = total
        return carry

    lax.fori_loop(lo, hi, one, 0)


def _kernel(
    field_hbm, modes_ref, rows_ref, pick_ref, mid_ref, coef_ref,
    first_hbm, second_hbm,
    field, terms_a, terms_b, low_a, low_b, high_a, high_b, lap,
    stage_a, stage_b, pool_a, pool_b, wf, wcat, mixed, out_a, out_b,
    local_sem, halo_send, halo_recv, send_sem, recv_sem,
):
    z = lax.axis_index("space")
    me = lax.axis_index("chaos")
    core = me % 2
    x = (me // 2) % SIDE
    y = me // (2 * SIDE)
    above = (z + 1) % SPACE
    below = (z + SPACE - 1) % SPACE
    has_low = z > 0
    has_high = z < SPACE - 1

    load = pltpu.make_async_copy(field_hbm, field, local_sem.at[0])
    load.start()

    peers = [
        (((y + dy) % SIDE) * SIDE + (x + dx) % SIDE) * 2 + (core + dc) % 2
        for dy, dx, dc in _offsets()
    ]
    barrier = pltpu.get_barrier_semaphore()
    for near in (above, below):
        pl.semaphore_signal(barrier, inc=1, device_id={"space": near}, device_id_type=MESH)
    for peer in peers:
        pl.semaphore_signal(barrier, inc=1, device_id={"chaos": peer}, device_id_type=MESH)

    load.wait()
    for g in range(GX):
        for p in range(PLANES):
            terms_a[g, p] = field[pl.ds(p * GX + g, TERMS, stride=CELL_ROWS), :]

    pl.semaphore_wait(barrier, AWAY + 2)

    def halo(apply, step, terms, low, high):
        lo, hi = HALO_STEPS[step]
        rows = pl.ds(lo, hi - lo)
        up = pltpu.make_async_remote_copy(
            src_ref=terms.at[rows, 1],
            dst_ref=low.at[rows],
            send_sem=halo_send.at[apply, step, 0],
            recv_sem=halo_recv.at[apply, step, 0],
            device_id={"space": above},
            device_id_type=MESH,
        )
        down = pltpu.make_async_remote_copy(
            src_ref=terms.at[rows, 0],
            dst_ref=high.at[rows],
            send_sem=halo_send.at[apply, step, 1],
            recv_sem=halo_recv.at[apply, step, 1],
            device_id={"space": below},
            device_id_type=MESH,
        )
        return up, down

    def exchange(slot, lo, hi, stage, pool):
        first_row, count = lo * PLANES, (hi - lo) * PLANES
        stage3 = stage.reshape(CELL_ROWS, POOL, GY)
        pool3 = pool.reshape(CELL_ROWS, POOL, GY)

        def entry(owner, c):
            term = rows_ref[0, owner * CAP + c]
            return lap[pl.ds(first_row * TERMS + term, count, stride=TERMS), :]

        for peer in peers:
            for c in range(CAP):
                at = first_row * POOL + peer * CAP + c
                stage[pl.ds(at, count, stride=POOL), :] = entry(peer, c)
            pltpu.make_async_remote_copy(
                src_ref=stage3.at[pl.ds(first_row, count), pl.ds(peer * CAP, CAP)],
                dst_ref=pool3.at[pl.ds(first_row, count), pl.ds(me * CAP, CAP)],
                send_sem=send_sem.at[slot],
                recv_sem=recv_sem.at[slot],
                device_id={"chaos": peer},
                device_id_type=MESH,
            ).start()
        for c in range(CAP):
            at = first_row * POOL + me * CAP + c
            pool[pl.ds(at, count, stride=POOL), :] = entry(me, c)

    def settle(slot, lo, hi, buffer, sem):
        part = buffer.reshape(CELL_ROWS, POOL, GY).at[
            pl.ds(lo * PLANES, (hi - lo) * PLANES), pl.ds(0, AWAY * CAP)
        ]
        pltpu.make_async_copy(part, part, sem.at[slot]).wait()

    halos = [halo(0, s, terms_a, low_a, high_a) for s in range(len(HALO_STEPS))]
    for pair in halos:
        for copy in pair:
            copy.start()
    for step, (lo, hi) in enumerate(FIRST_STEPS):
        for copy in halos[step]:
            copy.wait_recv()
        _laplace(lo, hi, low_a, high_a, has_low, has_high, terms_a, lap)
        exchange(step, lo, hi, stage_a, pool_a)

    _weights(pick_ref, mid_ref, coef_ref, wf, wcat)

    later = [halo(1, s, terms_b, low_b, high_b) for s in range(len(HALO_STEPS))]
    todo = list(enumerate(SECOND_STEPS, len(FIRST_STEPS)))
    for step, (lo, hi) in enumerate(FIRST_STEPS):
        settle(step, lo, hi, pool_a, recv_sem)
        _mix(lo, hi, pool_a, wcat, modes_ref, mixed, out_a, terms_b)
        for copy in later[step]:
            copy.start()
        for copy in later[step]:
            copy.wait_recv()
        ready = hi if hi == GX else hi - 1
        while todo and todo[0][1][1] <= ready:
            slot, (start, stop) = todo.pop(0)
            _laplace(start, stop, low_b, high_b, has_low, has_high, terms_b, lap)
            exchange(slot, start, stop, stage_b, pool_b)

    save_a = pltpu.make_async_copy(out_a, first_hbm, local_sem.at[1])
    save_a.start()
    for slot, (lo, hi) in enumerate(SECOND_STEPS, len(FIRST_STEPS)):
        settle(slot, lo, hi, pool_b, recv_sem)
        _mix(lo, hi, pool_b, wcat, modes_ref, mixed, out_b, None)
    save_b = pltpu.make_async_copy(out_b, second_hbm, local_sem.at[0])
    save_b.start()

    for step, (lo, hi) in enumerate(FIRST_STEPS):
        settle(step, lo, hi, stage_a, send_sem)
    for slot, (lo, hi) in enumerate(SECOND_STEPS, len(FIRST_STEPS)):
        settle(slot, lo, hi, stage_b, send_sem)
    for pair in halos + later:
        for copy in pair:
            copy.wait_send()
    save_a.wait()
    save_b.wait()


def per_device(field, modes, send_rows, pick, mode_ids, coef):
    flat = jax.ShapeDtypeStruct((TERMS * CELL_ROWS, GY), f32)
    vmem = pl.BlockSpec(memory_space=pltpu.VMEM)
    smem = pl.BlockSpec(memory_space=pltpu.SMEM)
    anywhere = pl.BlockSpec(memory_space=pl.ANY)
    steps = len(FIRST_STEPS) + len(SECOND_STEPS)
    first, second = pl.pallas_call(
        _kernel,
        out_shape=(flat, flat),
        in_specs=[anywhere, vmem, smem, vmem, vmem, vmem],
        out_specs=(anywhere, anywhere),
        name="galerkin",
        scratch_shapes=[
            pltpu.VMEM((TERMS * CELL_ROWS, GY), f32),
            *[pltpu.VMEM((GX, PLANES, TERMS, GY), f32)] * 2,
            *[pltpu.VMEM((GX, TERMS, GY), f32)] * 4,
            pltpu.VMEM((CELL_ROWS * TERMS, GY), f32),
            *[pltpu.VMEM((CELL_ROWS * POOL, GY), f32)] * 4,
            pltpu.VMEM((2, MODES_PAD * TERMS, GY), f32),
            pltpu.VMEM((W_ROWS, 3 * POOL), bf16),
            pltpu.VMEM((W_ROWS, PLANES * GY), f32),
            *[pltpu.VMEM((TERMS * CELL_ROWS, GY), f32)] * 2,
            pltpu.SemaphoreType.DMA((2,)),
            pltpu.SemaphoreType.DMA((2, len(HALO_STEPS), 2)),
            pltpu.SemaphoreType.DMA((2, len(HALO_STEPS), 2)),
            pltpu.SemaphoreType.DMA((steps,)),
            pltpu.SemaphoreType.DMA((steps,)),
        ],
        compiler_params=pltpu.CompilerParams(
            collective_id=0, has_side_effects=True, vmem_limit_bytes=40 << 20
        ),
    )(
        field.reshape(TERMS * CELL_ROWS, GY),
        modes.reshape(MODES * CELL_ROWS, GY),
        send_rows,
        pick,
        mode_ids,
        coef,
    )
    return first.reshape(field.shape), second.reshape(field.shape)


def solution(mesh):
    in_specs = (
        P("chaos", "space", None, None),
        P(None, "space", None, None),
        P("chaos", None),
        P("chaos", None),
        P("chaos", None),
        P("chaos", None),
    )
    out_specs = (P("chaos", "space", None, None), P("chaos", "space", None, None))
    return jax.shard_map(
        per_device, mesh=mesh, in_specs=in_specs, out_specs=out_specs, check_vma=False
    )
```

```python
import functools

import jax
import jax.numpy as jnp
from jax import lax
from jax.experimental import pallas as pl
from jax.experimental.pallas import tpu as pltpu
from jax.sharding import PartitionSpec as P

f32 = jnp.float32
bf16 = jnp.bfloat16
MESH = pl.DeviceIdType.MESH

SPACE = 16
OWNERS = 32
SIDE = 4
TERMS = 56
CAP = 8
POOL = OWNERS * CAP
SLOTS = 41
MODES = 21
MODES_PAD = 24
PLANES = 2
GX = 8
GY = 128
CELL_ROWS = GX * PLANES
BLOCKS = 3
GROUP = 19
W_ROWS = 1184
AWAY = OWNERS - 1

FIRST_STEPS = ((0, 2), (2, 5), (5, 8))
SECOND_STEPS = ((0, 1), (1, 4), (4, 6), (6, 8))


def _offsets():
    far = lambda n: min(n, SIDE - n)
    every = [
        (dy, dx, dc)
        for dy in range(SIDE)
        for dx in range(SIDE)
        for dc in range(2)
        if (dy, dx, dc) != (0, 0, 0)
    ]
    return sorted(every, key=lambda t: -(far(t[0]) + far(t[1])))


def _lanes(values):
    lane = lax.broadcasted_iota(jnp.int32, values.shape, 1)
    after = jnp.where(lane == GY - 1, 0.0, pltpu.roll(values, GY - 1, axis=1))
    before = jnp.where(lane == 0, 0.0, pltpu.roll(values, 1, axis=1))
    return after + before


def _laplace(lo, hi, low_ref, high_ref, terms, lap):
    for g in range(lo, hi):
        for p in range(PLANES):
            center = terms[g, p]
            outer = (high_ref if p else low_ref)[g]
            beside = terms[g, 1 - p] + outer + _lanes(center)
            if g > 0:
                beside = beside + terms[g - 1, p]
            if g < GX - 1:
                beside = beside + terms[g + 1, p]
            lap[pl.ds((g * PLANES + p) * TERMS, TERMS), :] = 6.0 * center - beside


def _weights(pick_ref, mid_ref, coef_ref, wf, wcat):
    lane = lax.broadcasted_iota(jnp.int32, (1, GY), 1)

    def side_by_side(ref, q, blocks):
        joined = ref[pl.ds(q, 1), :]
        for j in range(1, blocks):
            moved = pltpu.roll(ref[pl.ds(q + j * GROUP, 1), :], j * SLOTS, axis=1)
            joined = jnp.where(lane < j * SLOTS, joined, moved)
        return joined

    def rows(q, blocks):
        picked = side_by_side(pick_ref, q, blocks)
        mode = side_by_side(mid_ref, q, blocks)
        coef = side_by_side(coef_ref, q, blocks)
        n = MODES_PAD
        which = []
        for j in range(blocks):
            mine = (lane >= j * SLOTS) & (lane < (j + 1) * SLOTS)
            kind = jnp.where(mine, mode, -1)
            hit = lax.broadcasted_iota(jnp.int32, (n, GY), 0) == kind
            which.append(jnp.where(hit, coef, 0.0))
        which = jnp.concatenate(which, axis=0)
        place = jnp.where(
            lax.broadcasted_iota(jnp.int32, (POOL, GY), 0) == picked, 1.0, 0.0
        ).astype(bf16)
        top = which.astype(bf16)
        rest = which - top.astype(f32)
        mid = rest.astype(bf16)
        low = (rest - mid.astype(f32)).astype(bf16)
        parts = lax.dot_general(
            jnp.concatenate([top, mid, low], axis=0),
            place,
            (((1,), (1,)), ((), ())),
            preferred_element_type=f32,
        )
        m = n * blocks
        total = parts[0:m] + (parts[m : 2 * m] + parts[2 * m : 3 * m])
        for j in range(blocks):
            at = pl.ds(q + j * GROUP, n, stride=TERMS)
            wf[0, at, :] = total[j * n : (j + 1) * n, 0:128]
            wf[1, at, :] = total[j * n : (j + 1) * n, 128:256]

    def body(q, carry):
        rows(q, BLOCKS)
        return carry

    lax.fori_loop(0, GROUP - 1, body, 0)
    rows(GROUP - 1, BLOCKS - 1)

    def split(t, carry):
        at = pl.multiple_of(t * 16, 16)
        for h in range(2):
            w = wf[h, pl.ds(at, 16), :]
            top = w.astype(bf16)
            low = (w - top.astype(f32)).astype(bf16)
            wcat[pl.ds(at, 16), h * 128 : (h + 1) * 128] = top
            wcat[pl.ds(at, 16), POOL + h * 128 : POOL + (h + 1) * 128] = top
            wcat[pl.ds(at, 16), 2 * POOL + h * 128 : 2 * POOL + (h + 1) * 128] = low
        return carry

    lax.fori_loop(0, W_ROWS // 16, split, 0)


def _mix(lo, hi, pool, wcat, modes, mixed, out, terms, done=None):
    def one(g, carry):
        images = jnp.concatenate(
            [
                pool[pl.ds(pl.multiple_of(g * PLANES * POOL, POOL), POOL), :],
                pool[pl.ds(pl.multiple_of(g * PLANES * POOL + POOL, POOL), POOL), :],
            ],
            axis=1,
        )
        top = images.astype(bf16)
        low = (images - top.astype(f32)).astype(bf16)
        mixed[...] = jnp.dot(
            wcat[...], jnp.concatenate([top, low, top], axis=0), preferred_element_type=f32
        )
        for p in range(PLANES):
            total = None
            for k in range(MODES):
                scale = modes[pl.ds(k * CELL_ROWS + p * GX + g, 1), :]
                part = mixed[k * TERMS : (k + 1) * TERMS, p * GY : (p + 1) * GY] * scale
                total = part if total is None else total + part
            out[pl.ds(p * GX + g, TERMS, stride=CELL_ROWS), :] = total
            if terms is not None:
                terms[g, p] = total
        if done is not None:
            done(g)
        return carry

    lax.fori_loop(lo, hi, one, 0)


def _kernel(
    field_hbm, modes_hbm, rows_hbm, pick_hbm, mid_hbm, coef_hbm,
    first_hbm, second_hbm,
    field, modes_ref, rows_ref, pick_t, mid_t, coef_t, pick_ref, mid_ref, coef_ref, terms_a, terms_b, low_a, low_b, high_a, high_b, lap,
    stage_a, stage_b, pool_a, pool_b, wf, wcat, mixed, out_a, out_b,
    local_sem, halo_send, halo_recv, send_sem, recv_sem,
):
    z = lax.axis_index("space")
    me = lax.axis_index("chaos")
    core = me % 2
    x = (me // 2) % SIDE
    y = me // (2 * SIDE)
    above = (z + 1) % SPACE
    below = (z + SPACE - 1) % SPACE
    has_low = z > 0
    has_high = z < SPACE - 1

    pairs = (
        (field_hbm, field), (rows_hbm, rows_ref), (modes_hbm, modes_ref),
        (pick_hbm, pick_t), (mid_hbm, mid_t), (coef_hbm, coef_t),
    )
    loads = [
        pltpu.make_async_copy(source, target, local_sem.at[n])
        for n, (source, target) in enumerate(pairs)
    ]
    loads[0].start()

    peers = [
        (((y + dy) % SIDE) * SIDE + (x + dx) % SIDE) * 2 + (core + dc) % 2
        for dy, dx, dc in _offsets()
    ]
    barrier = pltpu.get_barrier_semaphore()
    for there, near in ((has_high, above), (has_low, below)):

        @pl.when(there)
        def _():
            pl.semaphore_signal(barrier, inc=1, device_id={"space": near}, device_id_type=MESH)

    for peer in peers:
        pl.semaphore_signal(barrier, inc=1, device_id={"chaos": peer}, device_id_type=MESH)

    for load in loads[1:]:
        load.start()

    @pl.when(z == 0)
    def _():
        low_a[...] = jnp.zeros_like(low_a)
        low_b[...] = jnp.zeros_like(low_b)

    @pl.when(z == SPACE - 1)
    def _():
        high_a[...] = jnp.zeros_like(high_a)
        high_b[...] = jnp.zeros_like(high_b)

    loads[0].wait()
    for g in range(GX):
        for p in range(PLANES):
            terms_a[g, p] = field[pl.ds(p * GX + g, TERMS, stride=CELL_ROWS), :]

    last = SPACE - 1
    slabs_beside = (z + last - 1) // last + (2 * last - 1 - z) // last
    pl.semaphore_wait(barrier, AWAY + slabs_beside)

    def halo(apply, step, terms, low, high, rows):
        up = pltpu.make_async_remote_copy(
            src_ref=terms.at[rows, 1],
            dst_ref=low.at[rows],
            send_sem=halo_send.at[apply, step, 0],
            recv_sem=halo_recv.at[apply, step, 0],
            device_id={"space": above},
            device_id_type=MESH,
        )
        down = pltpu.make_async_remote_copy(
            src_ref=terms.at[rows, 0],
            dst_ref=high.at[rows],
            send_sem=halo_send.at[apply, step, 1],
            recv_sem=halo_recv.at[apply, step, 1],
            device_id={"space": below},
            device_id_type=MESH,
        )
        return up, down

    def halo_start(pair):
        for there, copy in zip((has_high, has_low), pair):
            pl.when(there)(copy.start)

    def halo_arrive(pair):
        for there, copy in zip((has_low, has_high), pair):
            pl.when(there)(copy.wait_recv)

    def halo_leave(pair):
        for there, copy in zip((has_high, has_low), pair):
            pl.when(there)(copy.wait_send)

    def exchange(slot, lo, hi, stage, pool):
        first_row, count = lo * PLANES, (hi - lo) * PLANES
        stage3 = stage.reshape(CELL_ROWS, POOL, GY)
        pool3 = pool.reshape(CELL_ROWS, POOL, GY)

        def entry(owner, c):
            term = rows_ref[0, owner * CAP + c]
            return lap[pl.ds(first_row * TERMS + term, count, stride=TERMS), :]

        for peer in peers:
            for c in range(CAP):
                at = first_row * POOL + peer * CAP + c
                stage[pl.ds(at, count, stride=POOL), :] = entry(peer, c)
            pltpu.make_async_remote_copy(
                src_ref=stage3.at[pl.ds(first_row, count), pl.ds(peer * CAP, CAP)],
                dst_ref=pool3.at[pl.ds(first_row, count), pl.ds(me * CAP, CAP)],
                send_sem=send_sem.at[slot],
                recv_sem=recv_sem.at[slot],
                device_id={"chaos": peer},
                device_id_type=MESH,
            ).start()
        for c in range(CAP):
            at = first_row * POOL + me * CAP + c
            pool[pl.ds(at, count, stride=POOL), :] = entry(me, c)

    def settle(slot, lo, hi, buffer, sem):
        part = buffer.reshape(CELL_ROWS, POOL, GY).at[
            pl.ds(lo * PLANES, (hi - lo) * PLANES), pl.ds(0, AWAY * CAP)
        ]
        pltpu.make_async_copy(part, part, sem.at[slot]).wait()

    def all_rows(apply, terms, low, high):
        return [
            halo(apply, step, terms, low, high, pl.ds(lo, hi - lo))
            for step, (lo, hi) in enumerate(FIRST_STEPS)
        ]

    halos = all_rows(0, terms_a, low_a, high_a)
    later = all_rows(1, terms_b, low_b, high_b)
    for pair in halos:
        halo_start(pair)
    loads[1].wait()
    for step, (lo, hi) in enumerate(FIRST_STEPS):
        halo_arrive(halos[step])
        _laplace(lo, hi, low_a, high_a, terms_a, lap)
        exchange(step, lo, hi, stage_a, pool_a)

    for load in loads[2:]:
        load.wait()
    for source, target in ((pick_t, pick_ref), (mid_t, mid_ref), (coef_t, coef_ref)):
        target[...] = jnp.zeros_like(target)
        target[0:TERMS, 0:SLOTS] = jnp.transpose(source[...])
    _weights(pick_ref, mid_ref, coef_ref, wf, wcat)

    todo = list(enumerate(SECOND_STEPS, len(FIRST_STEPS)))
    for step, (lo, hi) in enumerate(FIRST_STEPS):
        settle(step, lo, hi, pool_a, recv_sem)

        def row_done(g):
            halo_start(halo(1, step, terms_b, low_b, high_b, pl.ds(g, 1)))

        _mix(lo, hi, pool_a, wcat, modes_ref, mixed, out_a, terms_b, row_done)
        halo_arrive(later[step])
        ready = hi if hi == GX else hi - 1
        while todo and todo[0][1][1] <= ready:
            slot, (start, stop) = todo.pop(0)
            _laplace(start, stop, low_b, high_b, terms_b, lap)
            exchange(slot, start, stop, stage_b, pool_b)

    save_a = pltpu.make_async_copy(out_a, first_hbm, local_sem.at[6])
    save_a.start()
    for slot, (lo, hi) in enumerate(SECOND_STEPS, len(FIRST_STEPS)):
        settle(slot, lo, hi, pool_b, recv_sem)
        _mix(lo, hi, pool_b, wcat, modes_ref, mixed, out_b, None)
    save_b = pltpu.make_async_copy(out_b, second_hbm, local_sem.at[7])
    save_b.start()

    for step, (lo, hi) in enumerate(FIRST_STEPS):
        settle(step, lo, hi, stage_a, send_sem)
    for slot, (lo, hi) in enumerate(SECOND_STEPS, len(FIRST_STEPS)):
        settle(slot, lo, hi, stage_b, send_sem)
    for pair in halos + later:
        halo_leave(pair)
    save_a.wait()
    save_b.wait()


def _save(first, second, first_out, second_out, held_first, held_second, sems):
    trips = ((second, held_second, second_out), (first, held_first, first_out))
    loads = [
        pltpu.make_async_copy(source, held, sems.at[n])
        for n, (source, held, _) in enumerate(trips)
    ]
    stores = [
        pltpu.make_async_copy(held, target, sems.at[2 + n])
        for n, (_, held, target) in enumerate(trips)
    ]
    for load in loads:
        load.start()
    for load, store in zip(loads, stores):
        load.wait()
        store.start()
    for store in stores:
        store.wait()


def per_device(field, modes, send_rows, pick, mode_ids, coef):
    flat = jax.ShapeDtypeStruct((TERMS * CELL_ROWS, GY), f32)
    hbm = pl.BlockSpec(memory_space=pltpu.HBM)
    steps = len(FIRST_STEPS) + len(SECOND_STEPS)
    first, second = pl.pallas_call(
        _kernel,
        out_shape=(flat, flat),
        in_specs=[hbm] * 6,
        out_specs=(hbm, hbm),
        name="galerkin",
        scratch_shapes=[
            pltpu.VMEM((TERMS * CELL_ROWS, GY), f32),
            pltpu.VMEM((MODES * CELL_ROWS, GY), f32),
            pltpu.SMEM((1, POOL), jnp.int32),
            *[pltpu.VMEM((SLOTS, TERMS), kind) for kind in (jnp.int32, jnp.int32, f32)],
            *[pltpu.VMEM((64, GY), kind) for kind in (jnp.int32, jnp.int32, f32)],
            *[pltpu.VMEM((GX, PLANES, TERMS, GY), f32)] * 2,
            *[pltpu.VMEM((GX, TERMS, GY), f32)] * 4,
            pltpu.VMEM((CELL_ROWS * TERMS, GY), f32),
            *[pltpu.VMEM((CELL_ROWS * POOL, GY), f32)] * 4,
            pltpu.VMEM((2, MODES_PAD * TERMS, GY), f32),
            pltpu.VMEM((W_ROWS, 3 * POOL), bf16),
            pltpu.VMEM((W_ROWS, PLANES * GY), f32),
            *[pltpu.VMEM((TERMS * CELL_ROWS, GY), f32)] * 2,
            pltpu.SemaphoreType.DMA((8,)),
            pltpu.SemaphoreType.DMA((2, len(FIRST_STEPS), 2)),
            pltpu.SemaphoreType.DMA((2, len(FIRST_STEPS), 2)),
            pltpu.SemaphoreType.DMA((steps,)),
            pltpu.SemaphoreType.DMA((steps,)),
        ],
        compiler_params=pltpu.CompilerParams(
            collective_id=0, has_side_effects=True, vmem_limit_bytes=60 << 20
        ),
    )(
        field.reshape(TERMS * CELL_ROWS, GY),
        modes.reshape(MODES * CELL_ROWS, GY),
        send_rows,
        pick.T,
        mode_ids.T,
        coef.T,
    )
    anywhere = pl.BlockSpec(memory_space=pl.ANY)
    first, second = pl.pallas_call(
        _save,
        out_shape=(flat, flat),
        in_specs=[anywhere] * 2,
        out_specs=(anywhere,) * 2,
        name="save",
        scratch_shapes=[
            *[pltpu.VMEM((TERMS * CELL_ROWS, GY), f32)] * 2,
            pltpu.SemaphoreType.DMA((4,)),
        ],
    )(first, second)
    return first.reshape(field.shape), second.reshape(field.shape)


def solution(mesh):
    in_specs = (
        P("chaos", "space", None, None),
        P(None, "space", None, None),
        P("chaos", None),
        P("chaos", None),
        P("chaos", None),
        P("chaos", None),
    )
    out_specs = (P("chaos", "space", None, None), P("chaos", "space", None, None))
    return jax.shard_map(
        per_device, mesh=mesh, in_specs=in_specs, out_specs=out_specs, check_vma=False
    )
```

```python
import functools

import jax
import jax.numpy as jnp
from jax import lax
from jax.experimental import pallas as pl
from jax.experimental.pallas import tpu as pltpu
from jax.sharding import PartitionSpec as P

f32 = jnp.float32
bf16 = jnp.bfloat16
MESH = pl.DeviceIdType.MESH

SPACE = 16
OWNERS = 32
SIDE = 4
TERMS = 56
CAP = 8
POOL = OWNERS * CAP
SLOTS = 41
MODES = 21
MODES_PAD = 24
PLANES = 2
GX = 8
GY = 128
CELL_ROWS = GX * PLANES
BLOCKS = 3
GROUP = 19
W_ROWS = 1184
AWAY = OWNERS - 1

FIRST_STEPS = ((0, 2), (2, 5), (5, 8))
SECOND_STEPS = ((0, 1), (1, 4), (4, 6), (6, 8))


def _offsets():
    far = lambda n: min(n, SIDE - n)
    every = [
        (dy, dx, dc)
        for dy in range(SIDE)
        for dx in range(SIDE)
        for dc in range(2)
        if (dy, dx, dc) != (0, 0, 0)
    ]
    return sorted(every, key=lambda t: -(far(t[0]) + far(t[1])))


def _lanes(values):
    lane = lax.broadcasted_iota(jnp.int32, values.shape, 1)
    after = jnp.where(lane == GY - 1, 0.0, pltpu.roll(values, GY - 1, axis=1))
    before = jnp.where(lane == 0, 0.0, pltpu.roll(values, 1, axis=1))
    return after + before


def _laplace(lo, hi, low_ref, high_ref, terms, lap):
    for g in range(lo, hi):
        for p in range(PLANES):
            center = terms[g, p]
            outer = (high_ref if p else low_ref)[g]
            beside = terms[g, 1 - p] + outer + _lanes(center)
            if g > 0:
                beside = beside + terms[g - 1, p]
            if g < GX - 1:
                beside = beside + terms[g + 1, p]
            lap[pl.ds((g * PLANES + p) * TERMS, TERMS), :] = 6.0 * center - beside


def _weights(pick_ref, mid_ref, coef_ref, wf, wcat):
    lane = lax.broadcasted_iota(jnp.int32, (1, GY), 1)

    def side_by_side(ref, q, blocks):
        joined = ref[pl.ds(q, 1), :]
        for j in range(1, blocks):
            moved = pltpu.roll(ref[pl.ds(q + j * GROUP, 1), :], j * SLOTS, axis=1)
            joined = jnp.where(lane < j * SLOTS, joined, moved)
        return joined

    def rows(q, blocks):
        picked = side_by_side(pick_ref, q, blocks)
        mode = side_by_side(mid_ref, q, blocks)
        coef = side_by_side(coef_ref, q, blocks)
        n = MODES_PAD
        which = []
        for j in range(blocks):
            mine = (lane >= j * SLOTS) & (lane < (j + 1) * SLOTS)
            kind = jnp.where(mine, mode, -1)
            hit = lax.broadcasted_iota(jnp.int32, (n, GY), 0) == kind
            which.append(jnp.where(hit, coef, 0.0))
        which = jnp.concatenate(which, axis=0)
        place = jnp.where(
            lax.broadcasted_iota(jnp.int32, (POOL, GY), 0) == picked, 1.0, 0.0
        ).astype(bf16)
        top = which.astype(bf16)
        rest = which - top.astype(f32)
        mid = rest.astype(bf16)
        low = (rest - mid.astype(f32)).astype(bf16)
        parts = lax.dot_general(
            jnp.concatenate([top, mid, low], axis=0),
            place,
            (((1,), (1,)), ((), ())),
            preferred_element_type=f32,
        )
        m = n * blocks
        total = parts[0:m] + (parts[m : 2 * m] + parts[2 * m : 3 * m])
        for j in range(blocks):
            at = pl.ds(q + j * GROUP, n, stride=TERMS)
            wf[0, at, :] = total[j * n : (j + 1) * n, 0:128]
            wf[1, at, :] = total[j * n : (j + 1) * n, 128:256]

    def body(q, carry):
        rows(q, BLOCKS)
        return carry

    lax.fori_loop(0, GROUP - 1, body, 0)
    rows(GROUP - 1, BLOCKS - 1)

    def split(t, carry):
        at = pl.multiple_of(t * 16, 16)
        for h in range(2):
            w = wf[h, pl.ds(at, 16), :]
            top = w.astype(bf16)
            low = (w - top.astype(f32)).astype(bf16)
            wcat[pl.ds(at, 16), h * 128 : (h + 1) * 128] = top
            wcat[pl.ds(at, 16), POOL + h * 128 : POOL + (h + 1) * 128] = top
            wcat[pl.ds(at, 16), 2 * POOL + h * 128 : 2 * POOL + (h + 1) * 128] = low
        return carry

    lax.fori_loop(0, W_ROWS // 16, split, 0)


def _mix(lo, hi, pool, wcat, modes, mixed, out, terms, done=None):
    def one(g, carry):
        images = jnp.concatenate(
            [
                pool[pl.ds(pl.multiple_of(g * PLANES * POOL, POOL), POOL), :],
                pool[pl.ds(pl.multiple_of(g * PLANES * POOL + POOL, POOL), POOL), :],
            ],
            axis=1,
        )
        top = images.astype(bf16)
        low = (images - top.astype(f32)).astype(bf16)
        mixed[...] = jnp.dot(
            wcat[...], jnp.concatenate([top, low, top], axis=0), preferred_element_type=f32
        )
        for p in range(PLANES):
            total = None
            for k in range(MODES):
                scale = modes[pl.ds(k * CELL_ROWS + p * GX + g, 1), :]
                part = mixed[k * TERMS : (k + 1) * TERMS, p * GY : (p + 1) * GY] * scale
                total = part if total is None else total + part
            out[pl.ds(p * GX + g, TERMS, stride=CELL_ROWS), :] = total
            if terms is not None:
                terms[g, p] = total
        if done is not None:
            done(g)
        return carry

    lax.fori_loop(lo, hi, one, 0)


def _kernel(
    field_hbm, modes_hbm, rows_hbm, pick_hbm, mid_hbm, coef_hbm,
    out_a, out_b,
    field, modes_ref, rows_ref, pick_t, mid_t, coef_t, pick_ref, mid_ref, coef_ref, terms_a, terms_b, low_a, low_b, high_a, high_b, lap,
    stage_a, stage_b, pool_a, pool_b, wf, wcat, mixed,
    local_sem, halo_send, halo_recv, send_sem, recv_sem,
):
    z = lax.axis_index("space")
    me = lax.axis_index("chaos")
    core = me % 2
    x = (me // 2) % SIDE
    y = me // (2 * SIDE)
    above = (z + 1) % SPACE
    below = (z + SPACE - 1) % SPACE
    has_low = z > 0
    has_high = z < SPACE - 1

    pairs = (
        (field_hbm, field), (rows_hbm, rows_ref), (modes_hbm, modes_ref),
        (pick_hbm, pick_t), (mid_hbm, mid_t), (coef_hbm, coef_t),
    )
    loads = [
        pltpu.make_async_copy(source, target, local_sem.at[n])
        for n, (source, target) in enumerate(pairs)
    ]
    loads[0].start()

    peers = [
        (((y + dy) % SIDE) * SIDE + (x + dx) % SIDE) * 2 + (core + dc) % 2
        for dy, dx, dc in _offsets()
    ]
    barrier = pltpu.get_barrier_semaphore()
    for there, near in ((has_high, above), (has_low, below)):

        @pl.when(there)
        def _():
            pl.semaphore_signal(barrier, inc=1, device_id={"space": near}, device_id_type=MESH)

    for peer in peers:
        pl.semaphore_signal(barrier, inc=1, device_id={"chaos": peer}, device_id_type=MESH)

    for load in loads[1:]:
        load.start()

    @pl.when(z == 0)
    def _():
        low_a[...] = jnp.zeros_like(low_a)
        low_b[...] = jnp.zeros_like(low_b)

    @pl.when(z == SPACE - 1)
    def _():
        high_a[...] = jnp.zeros_like(high_a)
        high_b[...] = jnp.zeros_like(high_b)

    loads[0].wait()
    for g in range(GX):
        for p in range(PLANES):
            terms_a[g, p] = field[pl.ds(p * GX + g, TERMS, stride=CELL_ROWS), :]

    last = SPACE - 1
    slabs_beside = (z + last - 1) // last + (2 * last - 1 - z) // last
    pl.semaphore_wait(barrier, AWAY + slabs_beside)

    def halo(apply, step, terms, low, high, rows):
        up = pltpu.make_async_remote_copy(
            src_ref=terms.at[rows, 1],
            dst_ref=low.at[rows],
            send_sem=halo_send.at[apply, step, 0],
            recv_sem=halo_recv.at[apply, step, 0],
            device_id={"space": above},
            device_id_type=MESH,
        )
        down = pltpu.make_async_remote_copy(
            src_ref=terms.at[rows, 0],
            dst_ref=high.at[rows],
            send_sem=halo_send.at[apply, step, 1],
            recv_sem=halo_recv.at[apply, step, 1],
            device_id={"space": below},
            device_id_type=MESH,
        )
        return up, down

    def halo_start(pair):
        for there, copy in zip((has_high, has_low), pair):
            pl.when(there)(copy.start)

    def halo_arrive(pair):
        for there, copy in zip((has_low, has_high), pair):
            pl.when(there)(copy.wait_recv)

    def halo_leave(pair):
        for there, copy in zip((has_high, has_low), pair):
            pl.when(there)(copy.wait_send)

    def exchange(slot, lo, hi, stage, pool):
        first_row, count = lo * PLANES, (hi - lo) * PLANES
        stage3 = stage.reshape(CELL_ROWS, POOL, GY)
        pool3 = pool.reshape(CELL_ROWS, POOL, GY)

        def entry(owner, c):
            term = rows_ref[0, owner * CAP + c]
            return lap[pl.ds(first_row * TERMS + term, count, stride=TERMS), :]

        for peer in peers:
            for c in range(CAP):
                at = first_row * POOL + peer * CAP + c
                stage[pl.ds(at, count, stride=POOL), :] = entry(peer, c)
            pltpu.make_async_remote_copy(
                src_ref=stage3.at[pl.ds(first_row, count), pl.ds(peer * CAP, CAP)],
                dst_ref=pool3.at[pl.ds(first_row, count), pl.ds(me * CAP, CAP)],
                send_sem=send_sem.at[slot],
                recv_sem=recv_sem.at[slot],
                device_id={"chaos": peer},
                device_id_type=MESH,
            ).start()
        for c in range(CAP):
            at = first_row * POOL + me * CAP + c
            pool[pl.ds(at, count, stride=POOL), :] = entry(me, c)

    def settle(slot, lo, hi, buffer, sem):
        part = buffer.reshape(CELL_ROWS, POOL, GY).at[
            pl.ds(lo * PLANES, (hi - lo) * PLANES), pl.ds(0, AWAY * CAP)
        ]
        pltpu.make_async_copy(part, part, sem.at[slot]).wait()

    def all_rows(apply, terms, low, high):
        return [
            halo(apply, step, terms, low, high, pl.ds(lo, hi - lo))
            for step, (lo, hi) in enumerate(FIRST_STEPS)
        ]

    halos = all_rows(0, terms_a, low_a, high_a)
    later = all_rows(1, terms_b, low_b, high_b)
    for pair in halos:
        halo_start(pair)
    loads[1].wait()
    for step, (lo, hi) in enumerate(FIRST_STEPS):
        halo_arrive(halos[step])
        _laplace(lo, hi, low_a, high_a, terms_a, lap)
        exchange(step, lo, hi, stage_a, pool_a)

    for load in loads[2:]:
        load.wait()
    for source, target in ((pick_t, pick_ref), (mid_t, mid_ref), (coef_t, coef_ref)):
        target[...] = jnp.zeros_like(target)
        target[0:TERMS, 0:SLOTS] = jnp.transpose(source[...])
    _weights(pick_ref, mid_ref, coef_ref, wf, wcat)

    todo = list(enumerate(SECOND_STEPS, len(FIRST_STEPS)))
    for step, (lo, hi) in enumerate(FIRST_STEPS):
        settle(step, lo, hi, pool_a, recv_sem)

        def row_done(g):
            halo_start(halo(1, step, terms_b, low_b, high_b, pl.ds(g, 1)))

        _mix(lo, hi, pool_a, wcat, modes_ref, mixed, out_a, terms_b, row_done)
        halo_arrive(later[step])
        ready = hi if hi == GX else hi - 1
        while todo and todo[0][1][1] <= ready:
            slot, (start, stop) = todo.pop(0)
            _laplace(start, stop, low_b, high_b, terms_b, lap)
            exchange(slot, start, stop, stage_b, pool_b)

    for slot, (lo, hi) in enumerate(SECOND_STEPS, len(FIRST_STEPS)):
        settle(slot, lo, hi, pool_b, recv_sem)
        _mix(lo, hi, pool_b, wcat, modes_ref, mixed, out_b, None)
    for step, (lo, hi) in enumerate(FIRST_STEPS):
        settle(step, lo, hi, stage_a, send_sem)
    for slot, (lo, hi) in enumerate(SECOND_STEPS, len(FIRST_STEPS)):
        settle(slot, lo, hi, stage_b, send_sem)
    for pair in halos + later:
        halo_leave(pair)


def _save(first, second, first_out, second_out, sems):
    copies = [
        pltpu.make_async_copy(first, first_out, sems.at[0]),
        pltpu.make_async_copy(second, second_out, sems.at[1]),
    ]
    for copy in copies:
        copy.start()
    for copy in copies:
        copy.wait()


def per_device(field, modes, send_rows, pick, mode_ids, coef):
    flat = jax.ShapeDtypeStruct((TERMS * CELL_ROWS, GY), f32)
    held = pltpu.VMEM((TERMS * CELL_ROWS, GY), f32)
    hbm = pl.BlockSpec(memory_space=pltpu.HBM)
    vmem = pl.BlockSpec(memory_space=pltpu.VMEM)
    steps = len(FIRST_STEPS) + len(SECOND_STEPS)
    first, second = pl.pallas_call(
        _kernel,
        out_shape=(held, held),
        in_specs=[hbm] * 6,
        out_specs=(vmem, vmem),
        name="galerkin",
        scratch_shapes=[
            pltpu.VMEM((TERMS * CELL_ROWS, GY), f32),
            pltpu.VMEM((MODES * CELL_ROWS, GY), f32),
            pltpu.SMEM((1, POOL), jnp.int32),
            *[pltpu.VMEM((SLOTS, TERMS), kind) for kind in (jnp.int32, jnp.int32, f32)],
            *[pltpu.VMEM((64, GY), kind) for kind in (jnp.int32, jnp.int32, f32)],
            *[pltpu.VMEM((GX, PLANES, TERMS, GY), f32)] * 2,
            *[pltpu.VMEM((GX, TERMS, GY), f32)] * 4,
            pltpu.VMEM((CELL_ROWS * TERMS, GY), f32),
            *[pltpu.VMEM((CELL_ROWS * POOL, GY), f32)] * 4,
            pltpu.VMEM((2, MODES_PAD * TERMS, GY), f32),
            pltpu.VMEM((W_ROWS, 3 * POOL), bf16),
            pltpu.VMEM((W_ROWS, PLANES * GY), f32),
            pltpu.SemaphoreType.DMA((8,)),
            pltpu.SemaphoreType.DMA((2, len(FIRST_STEPS), 2)),
            pltpu.SemaphoreType.DMA((2, len(FIRST_STEPS), 2)),
            pltpu.SemaphoreType.DMA((steps,)),
            pltpu.SemaphoreType.DMA((steps,)),
        ],
        compiler_params=pltpu.CompilerParams(
            collective_id=0, has_side_effects=True, vmem_limit_bytes=60 << 20
        ),
    )(
        field.reshape(TERMS * CELL_ROWS, GY),
        modes.reshape(MODES * CELL_ROWS, GY),
        send_rows,
        pick.T,
        mode_ids.T,
        coef.T,
    )
    first, second = pl.pallas_call(
        _save,
        out_shape=(flat, flat),
        in_specs=[pl.BlockSpec(memory_space=pl.ANY)] * 2,
        out_specs=(pl.BlockSpec(memory_space=pl.ANY),) * 2,
        name="save",
        scratch_shapes=[pltpu.SemaphoreType.DMA((2,))],
    )(*(pltpu.with_memory_space_constraint(part, pltpu.VMEM) for part in (first, second)))
    return first.reshape(field.shape), second.reshape(field.shape)


def solution(mesh):
    in_specs = (
        P("chaos", "space", None, None),
        P(None, "space", None, None),
        P("chaos", None),
        P("chaos", None),
        P("chaos", None),
        P("chaos", None),
    )
    out_specs = (P("chaos", "space", None, None), P("chaos", "space", None, None))
    return jax.shard_map(
        per_device, mesh=mesh, in_specs=in_specs, out_specs=out_specs, check_vma=False
    )
```

```python
import functools

import jax
import jax.numpy as jnp
from jax import lax
from jax.experimental import pallas as pl
from jax.experimental.pallas import tpu as pltpu
from jax.sharding import PartitionSpec as P

f32 = jnp.float32
bf16 = jnp.bfloat16
MESH = pl.DeviceIdType.MESH

SPACE = 16
OWNERS = 32
SIDE = 4
TERMS = 56
CAP = 8
POOL = OWNERS * CAP
SLOTS = 41
MODES = 21
MODES_PAD = 24
PLANES = 2
GX = 8
GY = 128
CELL_ROWS = GX * PLANES
BLOCKS = 3
EARLY = 9
GROUP = 19
W_ROWS = 1184
AWAY = OWNERS - 1

FIRST_STEPS = ((0, 1), (1, 3), (3, 6), (6, 8))
SECOND_STEPS = ((0, 2), (2, 5), (5, 7), (7, 8))


def _offsets():
    far = lambda n: min(n, SIDE - n)
    every = [
        (dy, dx, dc)
        for dy in range(SIDE)
        for dx in range(SIDE)
        for dc in range(2)
        if (dy, dx, dc) != (0, 0, 0)
    ]
    return sorted(every, key=lambda t: -(far(t[0]) + far(t[1])))


def _lanes(values):
    lane = lax.broadcasted_iota(jnp.int32, values.shape, 1)
    after = jnp.where(lane == GY - 1, 0.0, pltpu.roll(values, GY - 1, axis=1))
    before = jnp.where(lane == 0, 0.0, pltpu.roll(values, 1, axis=1))
    return after + before


def _laplace(lo, hi, low_ref, high_ref, terms, lap):
    for g in range(lo, hi):
        for p in range(PLANES):
            center = terms[g, p]
            outer = (high_ref if p else low_ref)[g]
            beside = terms[g, 1 - p] + outer + _lanes(center)
            if g > 0:
                beside = beside + terms[g - 1, p]
            if g < GX - 1:
                beside = beside + terms[g + 1, p]
            lap[pl.ds((g * PLANES + p) * TERMS, TERMS), :] = 6.0 * center - beside


def _weights(pick_ref, mid_ref, coef_ref, wf, start, stop):
    lane = lax.broadcasted_iota(jnp.int32, (1, GY), 1)

    def side_by_side(ref, q, blocks):
        joined = ref[pl.ds(q, 1), :]
        for j in range(1, blocks):
            moved = pltpu.roll(ref[pl.ds(q + j * GROUP, 1), :], j * SLOTS, axis=1)
            joined = jnp.where(lane < j * SLOTS, joined, moved)
        return joined

    def rows(q, blocks):
        picked = side_by_side(pick_ref, q, blocks)
        mode = side_by_side(mid_ref, q, blocks)
        coef = side_by_side(coef_ref, q, blocks)
        n = MODES_PAD
        which = []
        for j in range(blocks):
            mine = (lane >= j * SLOTS) & (lane < (j + 1) * SLOTS)
            kind = jnp.where(mine, mode, -1)
            hit = lax.broadcasted_iota(jnp.int32, (n, GY), 0) == kind
            which.append(jnp.where(hit, coef, 0.0))
        which = jnp.concatenate(which, axis=0)
        place = jnp.where(
            lax.broadcasted_iota(jnp.int32, (POOL, GY), 0) == picked, 1.0, 0.0
        ).astype(bf16)
        top = which.astype(bf16)
        rest = which - top.astype(f32)
        mid = rest.astype(bf16)
        low = (rest - mid.astype(f32)).astype(bf16)
        parts = lax.dot_general(
            jnp.concatenate([top, mid, low], axis=0),
            place,
            (((1,), (1,)), ((), ())),
            preferred_element_type=f32,
        )
        m = n * blocks
        total = parts[0:m] + (parts[m : 2 * m] + parts[2 * m : 3 * m])
        for j in range(blocks):
            at = pl.ds(q + j * GROUP, n, stride=TERMS)
            wf[0, at, :] = total[j * n : (j + 1) * n, 0:128]
            wf[1, at, :] = total[j * n : (j + 1) * n, 128:256]

    def body(q, carry):
        rows(q, BLOCKS)
        return carry

    lax.fori_loop(start, min(stop, GROUP - 1), body, 0)
    if stop == GROUP:
        rows(GROUP - 1, BLOCKS - 1)


def _halves(wf, wcat):
    def split(t, carry):
        at = pl.multiple_of(t * 16, 16)
        for h in range(2):
            w = wf[h, pl.ds(at, 16), :]
            top = w.astype(bf16)
            low = (w - top.astype(f32)).astype(bf16)
            wcat[pl.ds(at, 16), h * 128 : (h + 1) * 128] = top
            wcat[pl.ds(at, 16), POOL + h * 128 : POOL + (h + 1) * 128] = top
            wcat[pl.ds(at, 16), 2 * POOL + h * 128 : 2 * POOL + (h + 1) * 128] = low
        return carry

    lax.fori_loop(0, W_ROWS // 16, split, 0)


def _mix(lo, hi, pool, wcat, modes, mixed, out, terms, done=None):
    def one(g, carry):
        images = jnp.concatenate(
            [
                pool[pl.ds(pl.multiple_of(g * PLANES * POOL, POOL), POOL), :],
                pool[pl.ds(pl.multiple_of(g * PLANES * POOL + POOL, POOL), POOL), :],
            ],
            axis=1,
        )
        top = images.astype(bf16)
        low = (images - top.astype(f32)).astype(bf16)
        mixed[...] = jnp.dot(
            wcat[...], jnp.concatenate([top, low, top], axis=0), preferred_element_type=f32
        )
        for p in range(PLANES):
            total = None
            for k in range(MODES):
                scale = modes[pl.ds(k * CELL_ROWS + p * GX + g, 1), :]
                part = mixed[k * TERMS : (k + 1) * TERMS, p * GY : (p + 1) * GY] * scale
                total = part if total is None else total + part
            out[pl.ds(p * GX + g, TERMS, stride=CELL_ROWS), :] = total
            if terms is not None:
                terms[g, p] = total
        if done is not None:
            done(g)
        return carry

    lax.fori_loop(lo, hi, one, 0)


def _kernel(
    field_hbm, modes_hbm, rows_hbm, pick_hbm, mid_hbm, coef_hbm,
    out_a, out_b,
    field, modes_ref, rows_ref, pick_t, mid_t, coef_t, pick_ref, mid_ref, coef_ref, terms_a, terms_b, low_a, low_b, high_a, high_b, lap,
    stage_a, stage_b, pool_a, pool_b, wf, wcat, mixed,
    local_sem, halo_send, halo_recv, send_sem, recv_sem,
):
    z = lax.axis_index("space")
    me = lax.axis_index("chaos")
    core = me % 2
    x = (me // 2) % SIDE
    y = me // (2 * SIDE)
    above = (z + 1) % SPACE
    below = (z + SPACE - 1) % SPACE
    has_low = z > 0
    has_high = z < SPACE - 1

    pairs = (
        (field_hbm, field), (rows_hbm, rows_ref), (modes_hbm, modes_ref),
        (pick_hbm, pick_t), (mid_hbm, mid_t), (coef_hbm, coef_t),
    )
    loads = [
        pltpu.make_async_copy(source, target, local_sem.at[n])
        for n, (source, target) in enumerate(pairs)
    ]
    loads[0].start()

    peers = [
        (((y + dy) % SIDE) * SIDE + (x + dx) % SIDE) * 2 + (core + dc) % 2
        for dy, dx, dc in _offsets()
    ]
    barrier = pltpu.get_barrier_semaphore()
    for there, near in ((has_high, above), (has_low, below)):

        @pl.when(there)
        def _():
            pl.semaphore_signal(barrier, inc=1, device_id={"space": near}, device_id_type=MESH)

    for peer in peers:
        pl.semaphore_signal(barrier, inc=1, device_id={"chaos": peer}, device_id_type=MESH)

    for load in loads[1:]:
        load.start()

    @pl.when(z == 0)
    def _():
        low_a[...] = jnp.zeros_like(low_a)
        low_b[...] = jnp.zeros_like(low_b)

    @pl.when(z == SPACE - 1)
    def _():
        high_a[...] = jnp.zeros_like(high_a)
        high_b[...] = jnp.zeros_like(high_b)

    loads[0].wait()
    for g in range(GX):
        for p in range(PLANES):
            terms_a[g, p] = field[pl.ds(p * GX + g, TERMS, stride=CELL_ROWS), :]

    last = SPACE - 1
    slabs_beside = (z + last - 1) // last + (2 * last - 1 - z) // last
    pl.semaphore_wait(barrier, AWAY + slabs_beside)

    def halo(apply, step, terms, low, high, rows):
        up = pltpu.make_async_remote_copy(
            src_ref=terms.at[rows, 1],
            dst_ref=low.at[rows],
            send_sem=halo_send.at[apply, step, 0],
            recv_sem=halo_recv.at[apply, step, 0],
            device_id={"space": above},
            device_id_type=MESH,
        )
        down = pltpu.make_async_remote_copy(
            src_ref=terms.at[rows, 0],
            dst_ref=high.at[rows],
            send_sem=halo_send.at[apply, step, 1],
            recv_sem=halo_recv.at[apply, step, 1],
            device_id={"space": below},
            device_id_type=MESH,
        )
        return up, down

    def halo_start(pair):
        for there, copy in zip((has_high, has_low), pair):
            pl.when(there)(copy.start)

    def halo_arrive(pair):
        for there, copy in zip((has_low, has_high), pair):
            pl.when(there)(copy.wait_recv)

    def halo_leave(pair):
        for there, copy in zip((has_high, has_low), pair):
            pl.when(there)(copy.wait_send)

    def exchange(slot, lo, hi, stage, pool):
        first_row, count = lo * PLANES, (hi - lo) * PLANES
        stage3 = stage.reshape(CELL_ROWS, POOL, GY)
        pool3 = pool.reshape(CELL_ROWS, POOL, GY)

        def entry(owner, c):
            term = rows_ref[0, owner * CAP + c]
            return lap[pl.ds(first_row * TERMS + term, count, stride=TERMS), :]

        for peer in peers:
            for c in range(CAP):
                at = first_row * POOL + peer * CAP + c
                stage[pl.ds(at, count, stride=POOL), :] = entry(peer, c)
            pltpu.make_async_remote_copy(
                src_ref=stage3.at[pl.ds(first_row, count), pl.ds(peer * CAP, CAP)],
                dst_ref=pool3.at[pl.ds(first_row, count), pl.ds(me * CAP, CAP)],
                send_sem=send_sem.at[slot],
                recv_sem=recv_sem.at[slot],
                device_id={"chaos": peer},
                device_id_type=MESH,
            ).start()
        for c in range(CAP):
            at = first_row * POOL + me * CAP + c
            pool[pl.ds(at, count, stride=POOL), :] = entry(me, c)

    def settle(slot, lo, hi, buffer, sem):
        part = buffer.reshape(CELL_ROWS, POOL, GY).at[
            pl.ds(lo * PLANES, (hi - lo) * PLANES), pl.ds(0, AWAY * CAP)
        ]
        pltpu.make_async_copy(part, part, sem.at[slot]).wait()

    def all_rows(apply, terms, low, high):
        return [
            halo(apply, step, terms, low, high, pl.ds(lo, hi - lo))
            for step, (lo, hi) in enumerate(FIRST_STEPS)
        ]

    halos = all_rows(0, terms_a, low_a, high_a)
    later = all_rows(1, terms_b, low_b, high_b)
    for pair in halos:
        halo_start(pair)
    for load in loads[1:]:
        load.wait()
    for source, target in ((pick_t, pick_ref), (mid_t, mid_ref), (coef_t, coef_ref)):
        target[...] = jnp.zeros_like(target)
        target[0:TERMS, 0:SLOTS] = jnp.transpose(source[...])
    _weights(pick_ref, mid_ref, coef_ref, wf, 0, EARLY)
    for step, (lo, hi) in enumerate(FIRST_STEPS):
        halo_arrive(halos[step])
        _laplace(lo, hi, low_a, high_a, terms_a, lap)
        exchange(step, lo, hi, stage_a, pool_a)

    _weights(pick_ref, mid_ref, coef_ref, wf, EARLY, GROUP)
    _halves(wf, wcat)

    todo = list(enumerate(SECOND_STEPS, len(FIRST_STEPS)))
    for step, (lo, hi) in enumerate(FIRST_STEPS):
        settle(step, lo, hi, pool_a, recv_sem)

        def row_done(g):
            halo_start(halo(1, step, terms_b, low_b, high_b, pl.ds(g, 1)))

        _mix(lo, hi, pool_a, wcat, modes_ref, mixed, out_a, terms_b, row_done)
        halo_arrive(later[step])
        ready = hi if hi == GX else hi - 1
        while todo and todo[0][1][1] <= ready:
            slot, (start, stop) = todo.pop(0)
            _laplace(start, stop, low_b, high_b, terms_b, lap)
            exchange(slot, start, stop, stage_b, pool_b)

    for slot, (lo, hi) in enumerate(SECOND_STEPS, len(FIRST_STEPS)):
        settle(slot, lo, hi, pool_b, recv_sem)
        _mix(lo, hi, pool_b, wcat, modes_ref, mixed, out_b, None)
    for step, (lo, hi) in enumerate(FIRST_STEPS):
        settle(step, lo, hi, stage_a, send_sem)
    for slot, (lo, hi) in enumerate(SECOND_STEPS, len(FIRST_STEPS)):
        settle(slot, lo, hi, stage_b, send_sem)
    for pair in halos + later:
        halo_leave(pair)


def _save(first, second, first_out, second_out, sems):
    copies = [
        pltpu.make_async_copy(first, first_out, sems.at[0]),
        pltpu.make_async_copy(second, second_out, sems.at[1]),
    ]
    for copy in copies:
        copy.start()
    for copy in copies:
        copy.wait()


def per_device(field, modes, send_rows, pick, mode_ids, coef):
    flat = jax.ShapeDtypeStruct((TERMS * CELL_ROWS, GY), f32)
    held = pltpu.VMEM((TERMS * CELL_ROWS, GY), f32)
    hbm = pl.BlockSpec(memory_space=pltpu.HBM)
    vmem = pl.BlockSpec(memory_space=pltpu.VMEM)
    steps = len(FIRST_STEPS) + len(SECOND_STEPS)
    first, second = pl.pallas_call(
        _kernel,
        out_shape=(held, held),
        in_specs=[hbm] * 6,
        out_specs=(vmem, vmem),
        name="galerkin",
        scratch_shapes=[
            pltpu.VMEM((TERMS * CELL_ROWS, GY), f32),
            pltpu.VMEM((MODES * CELL_ROWS, GY), f32),
            pltpu.SMEM((1, POOL), jnp.int32),
            *[pltpu.VMEM((SLOTS, TERMS), kind) for kind in (jnp.int32, jnp.int32, f32)],
            *[pltpu.VMEM((64, GY), kind) for kind in (jnp.int32, jnp.int32, f32)],
            *[pltpu.VMEM((GX, PLANES, TERMS, GY), f32)] * 2,
            *[pltpu.VMEM((GX, TERMS, GY), f32)] * 4,
            pltpu.VMEM((CELL_ROWS * TERMS, GY), f32),
            *[pltpu.VMEM((CELL_ROWS * POOL, GY), f32)] * 4,
            pltpu.VMEM((2, MODES_PAD * TERMS, GY), f32),
            pltpu.VMEM((W_ROWS, 3 * POOL), bf16),
            pltpu.VMEM((W_ROWS, PLANES * GY), f32),
            pltpu.SemaphoreType.DMA((8,)),
            pltpu.SemaphoreType.DMA((2, len(FIRST_STEPS), 2)),
            pltpu.SemaphoreType.DMA((2, len(FIRST_STEPS), 2)),
            pltpu.SemaphoreType.DMA((steps,)),
            pltpu.SemaphoreType.DMA((steps,)),
        ],
        compiler_params=pltpu.CompilerParams(
            collective_id=0, has_side_effects=True, vmem_limit_bytes=60 << 20
        ),
    )(
        field.reshape(TERMS * CELL_ROWS, GY),
        modes.reshape(MODES * CELL_ROWS, GY),
        send_rows,
        pick.T,
        mode_ids.T,
        coef.T,
    )
    first, second = pl.pallas_call(
        _save,
        out_shape=(flat, flat),
        in_specs=[pl.BlockSpec(memory_space=pl.ANY)] * 2,
        out_specs=(pl.BlockSpec(memory_space=pl.ANY),) * 2,
        name="save",
        scratch_shapes=[pltpu.SemaphoreType.DMA((2,))],
    )(*(pltpu.with_memory_space_constraint(part, pltpu.VMEM) for part in (first, second)))
    return first.reshape(field.shape), second.reshape(field.shape)


def solution(mesh):
    in_specs = (
        P("chaos", "space", None, None),
        P(None, "space", None, None),
        P("chaos", None),
        P("chaos", None),
        P("chaos", None),
        P("chaos", None),
    )
    out_specs = (P("chaos", "space", None, None), P("chaos", "space", None, None))
    return jax.shard_map(
        per_device, mesh=mesh, in_specs=in_specs, out_specs=out_specs, check_vma=False
    )
```
